32 devices in a mesh: tile: 8 (over z, y), batch: 4 (over x, core).
Axes of the slice: x: 2, y: 2, z: 4, core: 2. Of those that a mesh axis runs over, the one named last changes fastest.
Arguments:
- transmission: float32 [2, 2, 512, 2048], P(None, None, 'tile'), may hold values from -4 to 4
- probe_modes: bfloat16 [4, 2, 128, 128], replicated, may hold values from -6 to 6
- amplitudes: float32 [8, 4, 12, 128, 128], P('tile', 'batch'), may hold values from 0.25 to 4
- positions: int32 [8, 4, 12, 2], P('tile', 'batch'), may hold values from -64 to 1920, as said below
- slot_counts: int32 [8, 4], P('tile', 'batch'), may hold values from 1 to 12, 24 in all within a row
Outputs:
- object_grad: float32 [2, 2, 512, 2048], P(None, None, 'tile', 'batch')
The draws below stay inside these ranges and needn't reach their ends.
Inputs may be any that keep to these rules, and one draw needn't show every extreme that they name: positions[t, b, i] = (r, c) with 64 t - 64 <= r < 64 t + 64 - 128 / 2 and 0 <= c <= 1920; dead slots hold positions in the same ranges. `slot_counts`: for every tile index t the counts of its 4 devices sum to exactly 24, and the largest of them is 12.
All inputs are finite; a program needn't handle non-finite values.
Results may differ from the reference program's by a relative error of at most 0.0084.
Values sent between devices are 32-bit elements; how exact they have to be, the bound alone decides.
No kernel may reach another device: no remote copies, remote signals or barrier semaphores. Data moves between devices by JAX's collectives and lax.ppermute only.
A program may use at most 64 MiB of HBM per device.

```python
import math
import jax
import jax.numpy as jnp
import numpy as np
from jax import lax

PATCH = 128
MODES = 4
SLICES = 2
STRIP = 64
OBJ_W = 2048
POS_AVG = 6
POS_MAX = 12
TILES = 8
BATCHES = 4
ROWS = 512


def draw_positions(key, part):
    row_key, col_key = jax.random.split(key)
    tile_ids = jnp.arange(TILES, dtype=jnp.int32)[:, None, None]
    offsets = jax.random.randint(row_key, (TILES, BATCHES, POS_MAX), 0, STRIP, dtype=jnp.int32)
    top_rows = tile_ids * STRIP - PATCH // 2 + offsets
    left_cols = jax.random.randint(col_key, (TILES, BATCHES, POS_MAX), 0, OBJ_W - PATCH + 1, dtype=jnp.int32)
    return jnp.stack([top_rows, left_cols], axis=-1).astype(jnp.int32)


def block_levels(rng, dims, shards, least, top_value):
    loudness = 1.0
    for dim, shards_of in shards:
        heights = jax.random.uniform(jax.random.fold_in(jax.random.fold_in(rng, 6), dim), (shards_of,), jnp.float32, least / len(shards), top_value / len(shards))
        loudness = loudness * jnp.repeat(jnp.exp(heights), dims[dim] // shards_of).reshape((-1,) + (1,) * (len(dims) - 1 - dim))
    return loudness


def split_up(count, total, most, skew):
    weights = [(1 << 20) // math.isqrt(standing ** skew) + 1 for standing in range(2, count + 1)]
    spare, holding = total - most - (count - 1), [1] * (count - 1)
    while spare > 0:
        candidates = [i for i in range(count - 1) if holding[i] < most]
        whole, left = sum([weights[i] for i in candidates]), spare
        for i in candidates:
            more = min(most - holding[i], max(1, left * weights[i] // whole), spare)
            holding[i] = holding[i] + more
            spare = spare - more
    return np.array([most] + holding)


def ragged_sizes(rng, number_of, total, bound, lean):
    if number_of == 2:
        one = jax.random.randint(rng, (), max(1, total - bound), min(bound, total - 1) + 1)
        return jnp.stack([one, total - one])
    lengths = jnp.asarray(split_up(number_of, total, bound, lean), jnp.int32)
    pairs = (number_of - 1) // 2
    donor, taker = lengths[1:1 + 2 * pairs:2], lengths[2:2 + 2 * pairs:2]
    slack = jnp.minimum(donor - 1, bound - taker)
    moved = jax.random.randint(jax.random.fold_in(rng, 1), (pairs,), 0, 1 << 20) % (slack + 1)
    lengths = lengths.at[1:1 + 2 * pairs:2].set(donor - moved).at[2:2 + 2 * pairs:2].set(taker + moved)
    return lengths[jax.random.permutation(jax.random.fold_in(rng, 2), number_of)]


def normal_values(rng, shape, scale, reach, cuts=(), held_as=jnp.bfloat16):
    values = scale * jax.random.normal(rng, shape, jnp.float32)
    if cuts:
        values = values * block_levels(rng, shape, cuts, -0.22, 0.18)
    return jnp.clip(values, -reach, reach).astype(held_as)


def setup_inputs(seed: int = 0) -> dict:
    keys = jax.random.split(jax.random.key(seed), 6)
    return {
        "transmission": normal_values(keys[0], (SLICES, 2, ROWS, OBJ_W), 0.7, 4.0, ((2, 8),), jnp.float32),
        "probe_modes": normal_values(keys[1], (MODES, 2, PATCH, PATCH), 1.0, 6.0),
        "amplitudes": jnp.clip(jnp.exp(math.log(4.0) - 2.7725887 * jax.random.uniform(keys[2], (TILES, BATCHES, POS_MAX, PATCH, PATCH), jnp.float32) ** block_levels(keys[2], (TILES, BATCHES, POS_MAX, PATCH, PATCH), ((0, 8), (1, 4)), -0.2, 0.2)), 0.25, 4.0),
        "positions": draw_positions(jax.random.fold_in(keys[5], 71), 0),
        "slot_counts": jax.vmap(lambda own: ragged_sizes(own, BATCHES, BATCHES * POS_AVG, POS_MAX, 0))(jax.random.split(keys[4], TILES)).reshape((TILES, BATCHES)).astype(jnp.int32),
    }


fresnel_phase = 3.0
amp_floor = 0.5
highest = lax.Precision.HIGHEST

def left_block(mat_re, mat_im):
    upper = jnp.concatenate([mat_re, -mat_im], axis=1)
    bottom = jnp.concatenate([mat_im, mat_re], axis=1)
    return jnp.concatenate([upper, bottom], axis=0).astype(jnp.bfloat16)

def right_block(mat_re, mat_im):
    from_re = jnp.stack([mat_re, mat_im], axis=1)
    from_im = jnp.stack([-mat_im, mat_re], axis=1)
    return jnp.stack([from_re, from_im], axis=0).astype(jnp.bfloat16)

def build_operators(patch_size):
    indices = jnp.arange(patch_size, dtype=jnp.int32)
    phase_index = indices[:, None] * indices[None, :] % patch_size
    angles = phase_index.astype(jnp.float32) * (2.0 * jnp.pi / patch_size)
    norm_scale = 1.0 / jnp.sqrt(jnp.float32(patch_size))
    four_re = jnp.cos(angles) * norm_scale
    four_im = -jnp.sin(angles) * norm_scale
    centred = jnp.where(indices < patch_size // 2, indices, indices - patch_size).astype(jnp.float32)
    scaled = centred / (patch_size // 2)
    kernel_phase = -fresnel_phase * scaled * scaled
    kern_re = jnp.cos(kernel_phase)
    kern_im = jnp.sin(kernel_phase)
    left_re = four_re * kern_re[None, :] + four_im * kern_im[None, :]
    left_im = four_re * kern_im[None, :] - four_im * kern_re[None, :]
    prop_re = jnp.dot(left_re, four_re, precision=highest) - jnp.dot(left_im, four_im, precision=highest)
    prop_im = jnp.dot(left_re, four_im, precision=highest) + jnp.dot(left_im, four_re, precision=highest)
    pairs = ((four_re, four_im), (four_re, -four_im), (prop_re, prop_im), (prop_re, -prop_im))
    return tuple(((left_block(p_re, p_im), right_block(p_re, p_im)) for p_re, p_im in pairs))

def apply_pair(pair, field):
    block, right = pair
    stacked = field.reshape(field.shape[0], 2 * field.shape[2], field.shape[3])
    partial_value = jnp.einsum('pq,nqc->npc', block.astype(jnp.float32), stacked.astype(jnp.float32))
    partial_value = partial_value.reshape(field.shape).astype(jnp.bfloat16)
    partial_value = lax.optimization_barrier(partial_value)
    return jnp.einsum('nerc,ecfd->nfrd', partial_value.astype(jnp.float32), right.astype(jnp.float32))

def complex_mul(a_re, a_im, b_re, b_im):
    return (a_re * b_re - a_im * b_im, a_re * b_im + a_im * b_re)

def conj_mul(a_re, a_im, b_re, b_im):
    return (a_re * b_re + a_im * b_im, a_re * b_im - a_im * b_re)

def slot_terms(operators, probe_modes, patches, amplitude):
    four, four_conj, prop, prop_conj = operators
    layers = patches.shape[0]
    probe_re = probe_modes[:, 0].astype(jnp.float32)
    probe_im = probe_modes[:, 1].astype(jnp.float32)
    wave_re, wave_im = complex_mul(probe_re, probe_im, patches[0, 0], patches[0, 1])
    wave = jnp.stack([wave_re, wave_im], axis=1).astype(jnp.bfloat16)
    carried = []
    for layer in range(1, layers):
        spread = apply_pair(prop, wave)
        carried.append(spread)
        wave_re, wave_im = complex_mul(spread[:, 0], spread[:, 1], patches[layer, 0], patches[layer, 1])
        wave = jnp.stack([wave_re, wave_im], axis=1).astype(jnp.bfloat16)
    far = apply_pair(four, wave)
    intensity = lax.optimization_barrier(jnp.sum(far * far, axis=(0, 1)))
    ratio = amplitude / jnp.maximum(jnp.sqrt(intensity), amp_floor)
    residual = (far * (1.0 - ratio)).astype(jnp.bfloat16)
    back = apply_pair(four_conj, residual)
    layer_terms = [None] * layers
    for layer in range(layers - 1, 0, -1):
        spread = carried[layer - 1]
        g_re, g_im = conj_mul(spread[:, 0], spread[:, 1], back[:, 0], back[:, 1])
        layer_terms[layer] = jnp.stack([lax.optimization_barrier(jnp.sum(g_re, axis=0)), lax.optimization_barrier(jnp.sum(g_im, axis=0))])
        b_re, b_im = conj_mul(patches[layer, 0], patches[layer, 1], back[:, 0], back[:, 1])
        back = apply_pair(prop_conj, jnp.stack([b_re, b_im], axis=1).astype(jnp.bfloat16))
    g_re, g_im = conj_mul(probe_re, probe_im, back[:, 0], back[:, 1])
    layer_terms[0] = jnp.stack([lax.optimization_barrier(jnp.sum(g_re, axis=0)), lax.optimization_barrier(jnp.sum(g_im, axis=0))])
    return jnp.stack(layer_terms)

def reference(transmission, probe_modes, amplitudes, positions, slot_counts):
    operators = build_operators(PATCH)
    half_size = PATCH // 2
    padded = jnp.pad(transmission, ((0, 0), (0, 0), (half_size, half_size), (0, 0)))
    counts = slot_counts.astype(jnp.int32)
    bounds = jnp.cumsum(counts, axis=1).astype(jnp.int32)
    starts = (bounds - counts).astype(jnp.int32)
    group_ids = jnp.arange(BATCHES * POS_AVG, dtype=jnp.int32)
    owners = lax.optimization_barrier(jnp.sum((bounds[:, None, :] <= group_ids[None, :, None]).astype(jnp.int32), axis=2)).astype(jnp.int32)
    first_slot = jnp.take_along_axis(starts, owners, axis=1).astype(jnp.int32)
    slot_ids = (group_ids[None, :] - first_slot).astype(jnp.int32)
    tile_ids = jnp.broadcast_to(jnp.arange(TILES, dtype=jnp.int32)[:, None], owners.shape)
    window = (SLICES, 2, PATCH, PATCH)

    def advance(gradient, slot_item):
        tile_id, owner, slot_id = slot_item
        amplitude = amplitudes[tile_id, owner, slot_id]
        top_row = (positions[tile_id, owner, slot_id, 0] + half_size).astype(jnp.int32)
        left_col = positions[tile_id, owner, slot_id, 1].astype(jnp.int32)
        corner = (jnp.int32(0), jnp.int32(0), top_row, left_col)
        patches = lax.dynamic_slice(padded, corner, window)
        pieces = slot_terms(operators, probe_modes, patches, amplitude)
        current = lax.dynamic_slice(gradient, corner, window)
        return (lax.dynamic_update_slice(gradient, current + pieces, corner), None)
    items = (tile_ids.reshape(-1), owners.reshape(-1), slot_ids.reshape(-1))
    gradient = lax.scan(advance, jnp.zeros(padded.shape, jnp.float32), items)[0]
    return gradient[:, :, half_size:half_size + ROWS]
```

```python
import functools

import jax
import jax.numpy as jnp
from jax import lax
from jax.experimental import pallas as pl
from jax.experimental.pallas import tpu as pltpu
from jax.sharding import PartitionSpec as P

fresnel_phase = 3.0
amp_floor = 0.5
highest = lax.Precision.HIGHEST


def build_operators(patch_size):
    indices = jnp.arange(patch_size, dtype=jnp.int32)
    phase_index = indices[:, None] * indices[None, :] % patch_size
    angles = phase_index.astype(jnp.float32) * (2.0 * jnp.pi / patch_size)
    norm_scale = 1.0 / jnp.sqrt(jnp.float32(patch_size))
    four_re = jnp.cos(angles) * norm_scale
    four_im = -jnp.sin(angles) * norm_scale
    centred = jnp.where(indices < patch_size // 2, indices, indices - patch_size).astype(
        jnp.float32
    )
    scaled = centred / (patch_size // 2)
    kernel_phase = -fresnel_phase * scaled * scaled
    kern_re = jnp.cos(kernel_phase)
    kern_im = jnp.sin(kernel_phase)
    left_re = four_re * kern_re[None, :] + four_im * kern_im[None, :]
    left_im = four_re * kern_im[None, :] - four_im * kern_re[None, :]
    prop_re = jnp.dot(left_re, four_re, precision=highest) - jnp.dot(
        left_im, four_im, precision=highest
    )
    prop_im = jnp.dot(left_re, four_im, precision=highest) + jnp.dot(
        left_im, four_re, precision=highest
    )

    def block(m_re, m_im):
        upper = jnp.concatenate([m_re, -m_im], axis=1)
        bottom = jnp.concatenate([m_im, m_re], axis=1)
        return jnp.concatenate([upper, bottom], axis=0)

    pairs = ((four_re, four_im), (four_re, -four_im), (prop_re, prop_im), (prop_re, -prop_im))
    return jnp.stack([block(a, b) for a, b in pairs]).astype(jnp.bfloat16)


def slot_kernel(
    meta,
    where_ref,
    ops_ref,
    probe_ref,
    above_ref,
    own_ref,
    below_ref,
    *rest,
    groups,
    slots,
    patch,
    modes,
    strip,
    quarter,
):
    amp_refs = rest[:groups]
    g_ref = rest[groups]
    ext, amps, probe, wave, spread, back, todo, sem = rest[groups + 1 :]
    p = patch
    half = p // 2
    copies = [
        pltpu.make_async_copy(above_ref, ext.at[:, pl.ds(0, half)], sem.at[0]),
        pltpu.make_async_copy(own_ref, ext.at[:, pl.ds(half, strip)], sem.at[1]),
        pltpu.make_async_copy(below_ref, ext.at[:, pl.ds(half + strip, half)], sem.at[2]),
    ]
    for j in range(groups):
        copies.append(
            pltpu.make_async_copy(
                amp_refs[j], amps.at[pl.ds(j * slots, slots)], sem.at[3 + j]
            )
        )
    for c in copies:
        c.start()
    g_ref[...] = jnp.zeros_like(g_ref)
    for m in range(modes):
        for q in range(2):
            probe[m, q] = probe_ref[m, q].astype(jnp.float32)
    base_row = where_ref[0]
    base_g = where_ref[1]
    base_o = where_ref[2]
    limit = where_ref[3]

    def scan_group(j, n):
        def scan_slot(i, n):
            col = meta[j, 1 + slots + i]
            mine = (col >= base_g) & (col < limit)
            todo[n] = j * slots + i
            return n + mine.astype(jnp.int32)

        return lax.fori_loop(0, meta[j, 0], scan_slot, n)

    count = lax.fori_loop(0, groups, scan_group, jnp.int32(0))
    for c in copies:
        c.wait()
    lane = lax.broadcasted_iota(jnp.int32, (p + 8, p), 1)
    sub = lax.broadcasted_iota(jnp.int32, (p // 8, 8, p), 1)
    win = ext.shape[2]

    def apply(left, right, out):
        for pair in range(0, modes, 2):
            y = jnp.dot(
                ops_ref[left],
                wave[:, pl.ds(pair * p, 2 * p)],
                preferred_element_type=jnp.float32,
            ).astype(jnp.bfloat16)
            for m in range(2):
                lhs = jnp.concatenate(
                    [y[:p, m * p : (m + 1) * p], y[p:, m * p : (m + 1) * p]], axis=1
                )
                out[pair + m] = jnp.dot(
                    lhs, ops_ref[right], preferred_element_type=jnp.float32
                )

    def body(k, carry):
        idx = todo[k]
        j = idx // slots
        i = idx - j * slots
        row = meta[j, 1 + i] - base_row
        col = meta[j, 1 + slots + i]
        lo = col - base_o
        lo0 = pl.multiple_of(jnp.minimum(lo // p, win // p - 2) * p, p)
        shift = lo - lo0
        lg = col - base_g
        lg0 = pl.multiple_of(lg // p * p, p)
        shift_g = lg - lg0
        unroll_by = lax.rem(2 * p - shift, p)

        row0 = pl.multiple_of(row // 8 * 8, 8)
        down = row - row0

        def obj(s):
            out = []
            for q in range(2):
                a = ext[2 * s + q, pl.ds(row0, p + 8), pl.ds(lo0, p)]
                b = ext[2 * s + q, pl.ds(row0, p + 8), pl.ds(lo0 + p, p)]
                x = pltpu.roll(jnp.where(lane >= shift, a, b), unroll_by, 1)
                x = x.reshape(p // 8 + 1, 8, p)
                x = pltpu.roll(x, lax.rem(8 - down, 8), 1)
                x = jnp.where(sub < 8 - down, x[:-1], x[1:])
                out.append(x.reshape(p, p))
            return out

        def emit(s, q, term):
            x = pltpu.roll(term, shift_g, 1).reshape(p // 8, 8, p)
            x = pltpu.roll(x, down, 1)
            first = jnp.where(sub >= down, x, 0.0)
            second = jnp.where(sub >= down, 0.0, x)
            zero = jnp.zeros((1, 8, p), jnp.float32)
            x = jnp.concatenate([first, zero]) + jnp.concatenate([zero, second])
            x = x.reshape(p + 8, p)
            left = jnp.where(lane >= shift_g, x, 0.0)
            right = jnp.where(lane >= shift_g, 0.0, x)
            g_ref[2 * s + q, pl.ds(row0, p + 8), pl.ds(lg0, p)] += left
            g_ref[2 * s + q, pl.ds(row0, p + 8), pl.ds(lg0 + p, p)] += right

        o_re, o_im = obj(0)
        for m in range(modes):
            a, b = probe[m, 0], probe[m, 1]
            wave[:p, pl.ds(m * p, p)] = (a * o_re - b * o_im).astype(jnp.bfloat16)
            wave[p:, pl.ds(m * p, p)] = (a * o_im + b * o_re).astype(jnp.bfloat16)
        apply(2, 3, spread)
        o_re, o_im = obj(1)
        for m in range(modes):
            a, b = spread[m, :, :p], spread[m, :, p:]
            wave[:p, pl.ds(m * p, p)] = (a * o_re - b * o_im).astype(jnp.bfloat16)
            wave[p:, pl.ds(m * p, p)] = (a * o_im + b * o_re).astype(jnp.bfloat16)
        apply(0, 1, back)
        intensity = jnp.zeros((p, p), jnp.float32)
        for m in range(modes):
            a, b = back[m, :, :p], back[m, :, p:]
            intensity = intensity + (a * a + b * b)
        ratio = amps[idx] / jnp.maximum(jnp.sqrt(intensity), amp_floor)
        factor = 1.0 - ratio
        for m in range(modes):
            wave[:p, pl.ds(m * p, p)] = (back[m, :, :p] * factor).astype(jnp.bfloat16)
            wave[p:, pl.ds(m * p, p)] = (back[m, :, p:] * factor).astype(jnp.bfloat16)
        apply(1, 0, back)
        t_re = jnp.zeros((p, p), jnp.float32)
        t_im = jnp.zeros((p, p), jnp.float32)
        for m in range(modes):
            a, b = spread[m, :, :p], spread[m, :, p:]
            c, d = back[m, :, :p], back[m, :, p:]
            t_re = t_re + (a * c + b * d)
            t_im = t_im + (a * d - b * c)
            wave[:p, pl.ds(m * p, p)] = (o_re * c + o_im * d).astype(jnp.bfloat16)
            wave[p:, pl.ds(m * p, p)] = (o_re * d - o_im * c).astype(jnp.bfloat16)
        emit(1, 0, t_re)
        emit(1, 1, t_im)
        apply(3, 2, back)
        t_re = jnp.zeros((p, p), jnp.float32)
        t_im = jnp.zeros((p, p), jnp.float32)
        for m in range(modes):
            a, b = probe[m, 0], probe[m, 1]
            c, d = back[m, :, :p], back[m, :, p:]
            t_re = t_re + (a * c + b * d)
            t_im = t_im + (a * d - b * c)
        emit(0, 0, t_re)
        emit(0, 1, t_im)
        return carry

    lax.fori_loop(0, count, body, 0)


def swapped(array, axis, bit):
    count = lax.axis_size(axis)
    return lax.ppermute(array, axis, [(i, i ^ bit) for i in range(count)])


def passed_along(array, axis, by):
    count = lax.axis_size(axis)
    pairs = [(i, i + by) for i in range(count) if 0 <= i + by < count]
    return lax.ppermute(array, axis, pairs)


def gathered(array, axis):
    count = lax.axis_size(axis)
    have = {0: array}
    bit = count // 2
    while bit:
        have.update({j | bit: swapped(a, axis, bit) for j, a in list(have.items())})
        bit //= 2
    return [have[j] for j in range(count)]


def on_device(transmission, probe_modes, amplitudes, positions, slot_counts):
    layers, parts, strip, width = transmission.shape
    modes = probe_modes.shape[0]
    patch = probe_modes.shape[-1]
    half = patch // 2
    slots = amplitudes.shape[2]
    groups = lax.axis_size("batch")
    b = lax.axis_index("batch")
    quarter = width // groups
    window = quarter + patch
    base_g = b * quarter
    base_o = jnp.minimum(base_g, width - window)
    planes = layers * parts
    local = lax.dynamic_slice_in_dim(
        transmission.reshape(planes, strip, width), base_o, window, axis=2
    )
    above = passed_along(local[:, strip - half :], "tile", 1)
    below = passed_along(local[:, :half], "tile", -1)
    meta = jnp.concatenate(
        [slot_counts.reshape(1), positions[0, 0, :, 0], positions[0, 0, :, 1]]
    ).astype(jnp.int32)
    metas = jnp.stack(gathered(meta, "batch"))
    amps = gathered(amplitudes[0, 0], "batch")
    operators = build_operators(patch)
    base_row = lax.axis_index("tile") * strip - half
    limit = jnp.where(b == groups - 1, width, base_g + quarter)
    where = jnp.stack([base_row, base_g, base_o, limit]).astype(jnp.int32)
    rows = strip + 2 * half
    vmem = pl.BlockSpec(memory_space=pltpu.VMEM)
    smem = pl.BlockSpec(memory_space=pltpu.SMEM)
    hbm = pl.BlockSpec(memory_space=pl.ANY)
    grad = pl.pallas_call(
        functools.partial(
            slot_kernel,
            groups=groups,
            slots=slots,
            patch=patch,
            modes=modes,
            strip=strip,
            quarter=quarter,
        ),
        out_shape=jax.ShapeDtypeStruct((planes, rows, window), jnp.float32),
        in_specs=[smem, smem, vmem, vmem, hbm, hbm, hbm] + [hbm] * groups,
        out_specs=vmem,
        scratch_shapes=[
            pltpu.VMEM((planes, rows, window), jnp.float32),
            pltpu.VMEM((groups * slots, patch, patch), jnp.float32),
            pltpu.VMEM((modes, 2, patch, patch), jnp.float32),
            pltpu.VMEM((2 * patch, modes * patch), jnp.bfloat16),
            pltpu.VMEM((modes, patch, 2 * patch), jnp.float32),
            pltpu.VMEM((modes, patch, 2 * patch), jnp.float32),
            pltpu.SMEM((groups * slots,), jnp.int32),
            pltpu.SemaphoreType.DMA((3 + groups,)),
        ],
        name="slots",
    )(metas, where, operators, probe_modes, above, local, below, *amps)
    over = passed_along(grad[:, :, quarter:], "batch", 1)
    merged = jnp.concatenate([grad[:, :, :patch] + over, grad[:, :, patch:quarter]], axis=2)
    from_above = passed_along(merged[:, half + strip :], "tile", 1)
    from_below = passed_along(merged[:, :half], "tile", -1)
    owned = merged[:, half : half + strip] + from_above + from_below
    return owned.reshape(layers, parts, strip, quarter)


def solution(mesh):
    return jax.shard_map(
        on_device,
        mesh=mesh,
        in_specs=(
            P(None, None, "tile", None),
            P(),
            P("tile", "batch", None, None, None),
            P("tile", "batch", None, None),
            P("tile", "batch"),
        ),
        out_specs=P(None, None, "tile", "batch"),
        check_vma=False,
    )
```

```python
import functools

import jax
import jax.numpy as jnp
from jax import lax
from jax.experimental import pallas as pl
from jax.experimental.pallas import tpu as pltpu
from jax.sharding import PartitionSpec as P

fresnel_phase = 3.0
amp_floor = 0.5
unroll = 4
highest = lax.Precision.HIGHEST


def build_operators(patch_size):
    indices = jnp.arange(patch_size, dtype=jnp.int32)
    phase_index = indices[:, None] * indices[None, :] % patch_size
    angles = phase_index.astype(jnp.float32) * (2.0 * jnp.pi / patch_size)
    norm_scale = 1.0 / jnp.sqrt(jnp.float32(patch_size))
    four_re = jnp.cos(angles) * norm_scale
    four_im = -jnp.sin(angles) * norm_scale
    centred = jnp.where(indices < patch_size // 2, indices, indices - patch_size).astype(
        jnp.float32
    )
    scaled = centred / (patch_size // 2)
    kernel_phase = -fresnel_phase * scaled * scaled
    kern_re = jnp.cos(kernel_phase)
    kern_im = jnp.sin(kernel_phase)
    left_re = four_re * kern_re[None, :] + four_im * kern_im[None, :]
    left_im = four_re * kern_im[None, :] - four_im * kern_re[None, :]
    prop_re = jnp.dot(left_re, four_re, precision=highest) - jnp.dot(
        left_im, four_im, precision=highest
    )
    prop_im = jnp.dot(left_re, four_im, precision=highest) + jnp.dot(
        left_im, four_re, precision=highest
    )

    def block(m_re, m_im):
        upper = jnp.concatenate([m_re, -m_im], axis=1)
        bottom = jnp.concatenate([m_im, m_re], axis=1)
        return jnp.concatenate([upper, bottom], axis=0)

    pairs = ((four_re, four_im), (four_re, -four_im), (prop_re, prop_im), (prop_re, -prop_im))
    return jnp.stack([block(a, b) for a, b in pairs]).astype(jnp.bfloat16)


def slot_kernel(meta, where_ref, ops_ref, probe_ref, own_ref, *rest, sizes):
    halo_rows, amp_cuts, groups, patch, modes, strip, quarter = sizes
    p = patch
    half = p // 2
    n_halo = len(halo_rows)
    n_amp = len(amp_cuts)
    slots = sum(amp_cuts)
    near_refs, rest = rest[:n_halo], rest[n_halo:]
    far_refs, rest = rest[:n_halo], rest[n_halo:]
    amp_refs, rest = rest[: groups * n_amp], rest[groups * n_amp :]
    over_out, above_out, below_out, first_out, own_out = rest[:5]
    ext, g_ref, amps, probe, o, fac, x, spread, back, todo, sem, amp_sem = rest[5:]
    rows = strip + 2 * half
    near_at = where_ref[4]
    far_at = where_ref[5]
    copies = [pltpu.make_async_copy(own_ref, ext.at[:, pl.ds(half, strip)], sem.at[0])]
    done = 0
    for c, size in enumerate(halo_rows):
        for side, (refs, at) in enumerate(((near_refs, near_at), (far_refs, far_at))):
            to = ext.at[:, pl.ds(pl.multiple_of(at + done, 8), size)]
            copies.append(pltpu.make_async_copy(refs[c], to, sem.at[1 + 2 * c + side]))
        done += size
    for c in copies:
        c.start()
    base_row = where_ref[0]
    base_g = where_ref[1]
    base_o = where_ref[2]
    limit = where_ref[3]

    count = jnp.int32(0)
    for j in range(groups):
        begin = 0
        for c, size in enumerate(amp_cuts):
            source = amp_refs[j * n_amp + c]

            def scan_slot(i, n, j=j, source=source, begin=begin):
                col = meta[j, 1 + slots + i]
                mine = (col >= base_g) & (col < limit)
                todo[n] = j * slots + i

                @pl.when(mine)
                def _():
                    pltpu.make_async_copy(
                        source.at[i - begin], amps.at[n], amp_sem.at[n]
                    ).start()

                return n + mine.astype(jnp.int32)

            end = jnp.clip(meta[j, 0], begin, begin + size)
            count = lax.fori_loop(begin, end, scan_slot, count)
            begin += size
    g_ref[...] = jnp.zeros_like(g_ref)
    for m in range(modes):
        for q in range(2):
            probe[m, q] = probe_ref[m, q].astype(jnp.float32)
    for c in copies:
        c.wait()

    def wait_amp(n, carry):
        pltpu.make_async_copy(amp_refs[0].at[0], amps.at[n], amp_sem.at[n]).wait()
        return carry

    lax.fori_loop(0, count, wait_amp, 0)
    lane = lax.broadcasted_iota(jnp.int32, (p + 8, p), 1)
    sub = lax.broadcasted_iota(jnp.int32, (p // 8, 8, p), 1)
    win = ext.shape[2]

    pairs = [tuple(range(m, min(m + 2, modes))) for m in range(0, modes, 2)]

    def stacked(fields):
        return jnp.concatenate(
            [
                jnp.concatenate([re.astype(jnp.bfloat16) for re, _ in fields], axis=1),
                jnp.concatenate([im.astype(jnp.bfloat16) for _, im in fields], axis=1),
            ],
            axis=0,
        )

    def apply(left, right, x):
        n = x.shape[1] // p
        y = jnp.dot(ops_ref[left], x, preferred_element_type=jnp.float32).astype(jnp.bfloat16)
        lhs = jnp.concatenate(
            [
                jnp.concatenate(
                    [y[:p, m * p : (m + 1) * p], y[p:, m * p : (m + 1) * p]], axis=1
                )
                for m in range(n)
            ],
            axis=0,
        )
        z = jnp.dot(lhs, ops_ref[right], preferred_element_type=jnp.float32)
        return [(z[m * p : (m + 1) * p, :p], z[m * p : (m + 1) * p, p:]) for m in range(n)]

    def work(u, k):
        valid = k < count
        last = jnp.minimum(k, count - 1)
        idx = todo[last]
        j = idx // slots
        i = idx - j * slots
        row = meta[j, 1 + i] - base_row
        col = meta[j, 1 + slots + i]
        lo = col - base_o
        lo0 = pl.multiple_of(jnp.minimum(lo // p, win // p - 2) * p, p)
        shift = lo - lo0
        lg = col - base_g
        lg0 = pl.multiple_of(lg // p * p, p)
        shift_g = lg - lg0
        left_from = jnp.where(valid, shift_g, p)
        right_to = jnp.where(valid, shift_g, 0)
        unroll_by = lax.rem(2 * p - shift, p)
        row0 = pl.multiple_of(row // 8 * 8, 8)
        down = row - row0

        def obj(s, q):
            a = ext[2 * s + q, pl.ds(row0, p + 8), pl.ds(lo0, p)]
            b = ext[2 * s + q, pl.ds(row0, p + 8), pl.ds(lo0 + p, p)]
            x = pltpu.roll(jnp.where(lane >= shift, a, b), unroll_by, 1)
            x = x.reshape(p // 8 + 1, 8, p)
            x = pltpu.roll(x, lax.rem(8 - down, 8), 1)
            x = jnp.where(sub < 8 - down, x[:-1], x[1:])
            o[u, s, q] = x.reshape(p, p)

        def emit(s, q, term):
            x = pltpu.roll(term, shift_g, 1).reshape(p // 8, 8, p)
            x = pltpu.roll(x, down, 1)
            first = jnp.where(sub >= down, x, 0.0)
            second = jnp.where(sub >= down, 0.0, x)
            zero = jnp.zeros((1, 8, p), jnp.float32)
            x = jnp.concatenate([first, zero]) + jnp.concatenate([zero, second])
            x = x.reshape(p + 8, p)
            left = jnp.where(lane >= left_from, x, 0.0)
            right = jnp.where(lane < right_to, x, 0.0)
            g_ref[2 * s + q, pl.ds(row0, p + 8), pl.ds(lg0, p)] += left
            g_ref[2 * s + q, pl.ds(row0, p + 8), pl.ds(lg0 + p, p)] += right

        def put(ref, n, fields):
            for m, (a, b) in zip(pairs[n], fields):
                ref[u, m, 0] = a
                ref[u, m, 1] = b

        def get(ref, n):
            return [(ref[u, m, 0], ref[u, m, 1]) for m in pairs[n]]

        def product(n, s):
            o_re, o_im = o[u, s, 0], o[u, s, 1]
            src = get(spread, n) if s else [(probe[m, 0], probe[m, 1]) for m in pairs[n]]
            return [(a * o_re - b * o_im, a * o_im + b * o_re) for a, b in src]

        for q in range(2):
            obj(0, q)
        for n in range(len(pairs)):
            x[u, n] = stacked(product(n, 0))
        yield
        for n in range(len(pairs)):
            put(spread, n, apply(2, 3, x[u, n]))
        yield
        for q in range(2):
            obj(1, q)
        for n in range(len(pairs)):
            x[u, n] = stacked(product(n, 1))
        yield
        for n in range(len(pairs)):
            put(back, n, apply(0, 1, x[u, n]))
        yield
        intensity = jnp.zeros((p, p), jnp.float32)
        for n in range(len(pairs)):
            for a, b in get(back, n):
                intensity = intensity + (a * a + b * b)
        ratio = amps[last] / jnp.maximum(jnp.sqrt(intensity), amp_floor)
        fac[u] = 1.0 - ratio
        for n in range(len(pairs)):
            x[u, n] = stacked([(a * fac[u], b * fac[u]) for a, b in get(back, n)])
        yield
        for n in range(len(pairs)):
            put(back, n, apply(1, 0, x[u, n]))
        yield
        t_re = jnp.zeros((p, p), jnp.float32)
        t_im = jnp.zeros((p, p), jnp.float32)
        o_re, o_im = o[u, 1, 0], o[u, 1, 1]
        for n in range(len(pairs)):
            nxt = []
            for (a, b), (c, d) in zip(get(spread, n), get(back, n)):
                t_re = t_re + (a * c + b * d)
                t_im = t_im + (a * d - b * c)
                nxt.append((o_re * c + o_im * d, o_re * d - o_im * c))
            x[u, n] = stacked(nxt)
        emit(1, 0, t_re)
        emit(1, 1, t_im)
        yield
        for n in range(len(pairs)):
            put(back, n, apply(3, 2, x[u, n]))
        yield
        t_re = jnp.zeros((p, p), jnp.float32)
        t_im = jnp.zeros((p, p), jnp.float32)
        for n in range(len(pairs)):
            for m, (c, d) in zip(pairs[n], get(back, n)):
                a, b = probe[m, 0], probe[m, 1]
                t_re = t_re + (a * c + b * d)
                t_im = t_im + (a * d - b * c)
        emit(0, 0, t_re)
        emit(0, 1, t_im)

    def run(start, width):
        steps = [work(u, start + u) for u in range(width)]
        live = list(range(width))
        tick = 0
        while live:
            for u in list(live):
                if tick >= u:
                    try:
                        next(steps[u])
                    except StopIteration:
                        live.remove(u)
            tick += 1

    def full(k, carry):
        run(unroll * k, unroll)
        return carry

    blocks = (count + 1) // unroll
    lax.fori_loop(0, blocks, full, 0)

    @pl.when(count > unroll * blocks)
    def _():
        run(unroll * blocks, unroll // 2)

    top = pl.ds(0, half)
    middle = pl.ds(half, strip)
    low = pl.ds(half + strip, half)
    main = pl.ds(p, quarter - p)
    outs = [
        pltpu.make_async_copy(g_ref.at[:, :, pl.ds(quarter, p)], over_out, sem.at[0]),
        pltpu.make_async_copy(g_ref.at[:, top, main], above_out, sem.at[1]),
        pltpu.make_async_copy(g_ref.at[:, low, main], below_out, sem.at[2]),
        pltpu.make_async_copy(g_ref.at[:, :, pl.ds(0, p)], first_out, sem.at[3]),
        pltpu.make_async_copy(g_ref.at[:, middle, main], own_out, sem.at[4]),
    ]
    for c in outs:
        c.start()
    for c in outs:
        c.wait()


def kernel_call(metas, where, operators, probe_modes, local, near, far, amps):
    planes, strip, window = local.shape
    modes, _, patch, _ = probe_modes.shape
    groups = len(amps)
    quarter = window - patch
    half = patch // 2
    rows = strip + 2 * half
    halo_rows = tuple(a.shape[1] for a in near)
    amp_cuts = tuple(a.shape[0] for a in amps[0])
    slots = sum(amp_cuts)
    sizes = (halo_rows, amp_cuts, groups, patch, modes, strip, quarter)
    vmem = pl.BlockSpec(memory_space=pltpu.VMEM)
    smem = pl.BlockSpec(memory_space=pltpu.SMEM)
    hbm = pl.BlockSpec(memory_space=pl.ANY)
    flat = [*near, *far] + [a for cuts in amps for a in cuts]

    def shape(*dims):
        return jax.ShapeDtypeStruct((planes,) + dims, jnp.float32)

    return pl.pallas_call(
        functools.partial(slot_kernel, sizes=sizes),
        out_shape=(
            shape(rows, patch),
            shape(half, quarter - patch),
            shape(half, quarter - patch),
            shape(rows, patch),
            shape(strip, quarter - patch),
        ),
        in_specs=[smem, smem, vmem, vmem] + [hbm] * (1 + len(flat)),
        out_specs=(hbm,) * 5,
        scratch_shapes=[
            pltpu.VMEM((planes, rows, window), jnp.float32),
            pltpu.VMEM((planes, rows, window), jnp.float32),
            pltpu.VMEM((groups * slots, patch, patch), jnp.float32),
            pltpu.VMEM((modes, 2, patch, patch), jnp.float32),
            pltpu.VMEM((unroll, 2, 2, patch, patch), jnp.float32),
            pltpu.VMEM((unroll, patch, patch), jnp.float32),
            pltpu.VMEM((unroll, modes // 2, 2 * patch, 2 * patch), jnp.bfloat16),
            pltpu.VMEM((unroll, modes, 2, patch, patch), jnp.float32),
            pltpu.VMEM((unroll, modes, 2, patch, patch), jnp.float32),
            pltpu.SMEM((groups * slots + 1,), jnp.int32),
            pltpu.SemaphoreType.DMA((max(5, 1 + 2 * len(halo_rows)),)),
            pltpu.SemaphoreType.DMA((groups * slots,)),
        ],
        name="slots",
    )(metas, where, operators, probe_modes, local, *flat)


def swapped(array, axis, bit):
    count = lax.axis_size(axis)
    return lax.ppermute(array, axis, [(i, i ^ bit) for i in range(count)])


def passed_along(array, axis, by):
    count = lax.axis_size(axis)
    pairs = [(i, i + by) for i in range(count) if 0 <= i + by < count]
    return lax.ppermute(array, axis, pairs)


def doubled(array, axis):
    array = array[None]
    bit = 1
    while bit < lax.axis_size(axis):
        array = jnp.concatenate([array, swapped(array, axis, bit)])
        bit *= 2
    return array


def gathered(array, axis):
    have = {0: array}
    bit = lax.axis_size(axis) // 2
    while bit:
        have.update({j | bit: swapped(a, axis, bit) for j, a in list(have.items())})
        bit //= 2
    return [have[j] for j in range(len(have))]


def forwarded(array, axis):
    count = lax.axis_size(axis)
    pairs = [(i, i + 2 - 4 * (i % 2)) for i in range(count)]
    return lax.ppermute(array, axis, [(i, k) for i, k in pairs if 0 <= k < count])


def halos(local, cuts):
    even = lax.axis_index("tile") % 2 == 0
    near, far = [], []
    at = 0
    for size in cuts[:-1]:
        piece = lax.slice_in_dim(local, at, at + size, axis=1)
        near.append(swapped(piece, "tile", 1))
        at += size
    for piece in near:
        far.append(forwarded(piece, "tile"))
    piece = lax.slice_in_dim(local, at, at + cuts[-1], axis=1)
    count = lax.axis_size("tile")
    near.append(swapped(piece, "tile", 1))
    pairs = [(i, i - 1 + 2 * (i % 2)) for i in range(count)]
    far.append(lax.ppermute(piece, "tile", [(i, k) for i, k in pairs if 0 <= k < count]))
    return near, far


def on_device(transmission, probe_modes, amplitudes, positions, slot_counts):
    layers, parts, strip, width = transmission.shape
    patch = probe_modes.shape[-1]
    half = patch // 2
    slots = amplitudes.shape[2]
    groups = lax.axis_size("batch")
    b = lax.axis_index("batch")
    t = lax.axis_index("tile")
    quarter = width // groups
    window = quarter + patch
    base_g = b * quarter
    base_o = jnp.minimum(base_g, width - window)
    planes = layers * parts
    split = slots - slots // 3
    pieces = [gathered(a, "batch") for a in (amplitudes[0, 0, :split], amplitudes[0, 0, split:])]
    amps = list(zip(*pieces))
    local = lax.dynamic_slice_in_dim(
        transmission.reshape(planes, strip, width), base_o, window, axis=2
    )
    near, far = halos(local, (half // 2, half // 4, half // 4))
    meta = jnp.concatenate(
        [slot_counts.reshape(1), positions[0, 0, :, 0], positions[0, 0, :, 1]]
    ).astype(jnp.int32)
    metas = doubled(meta, "batch")
    operators = build_operators(patch)
    base_row = t * strip - half
    limit = jnp.where(b == groups - 1, width, base_g + quarter)
    up = jnp.where(t % 2 == 0, half + strip, 0)
    down = half + strip - up
    where = jnp.stack([base_row, base_g, base_o, limit, up, down]).astype(jnp.int32)
    over, above, below, first, own = kernel_call(
        metas, where, operators, probe_modes, local, near, far, amps
    )
    over = passed_along(over, "batch", 1)
    from_above = passed_along(below, "tile", 1)
    from_below = passed_along(above, "tile", -1)
    first = first + over
    edge_above = passed_along(first[:, half + strip :], "tile", 1)
    edge_below = passed_along(first[:, :half], "tile", -1)
    owned = jnp.concatenate(
        [
            first[:, half : half + strip] + edge_above + edge_below,
            own + from_above + from_below,
        ],
        axis=2,
    )
    return owned.reshape(layers, parts, strip, quarter)


def solution(mesh):
    return jax.shard_map(
        on_device,
        mesh=mesh,
        in_specs=(
            P(None, None, "tile", None),
            P(),
            P("tile", "batch", None, None, None),
            P("tile", "batch", None, None),
            P("tile", "batch"),
        ),
        out_specs=P(None, None, "tile", "batch"),
        check_vma=False,
    )
```
